32 devices in a mesh: layer: 8 (over z, x), panel: 4 (over y, core).
Axes of the slice: x: 2, y: 2, z: 4, core: 2. Of those that a mesh axis runs over, the one named last changes fastest.
Arguments:
- lower_blocks: bfloat16 [8, 512, 512], P('layer', 'panel'), may hold values from -2 to 0.5
- diag_blocks: bfloat16 [8, 512, 512], P('layer', 'panel'), may hold values from -0.5 to 4, as said below
- upper_blocks: bfloat16 [8, 512, 512], P('layer', 'panel'), may hold values from -2 to 0.5
- right_sides: bfloat16 [8, 512, 128], P('layer', 'panel'), may hold values from -6 to 6
Outputs:
- reduced_diag: bfloat16 [8, 512, 512], P('layer', 'panel')
- reduced_rhs: bfloat16 [8, 512, 128], P('layer', 'panel')
The draws below stay inside these ranges and needn't reach their ends.
Inputs may be any that keep to these rules, and one draw needn't show every extreme that they name: `diag_blocks`: the diagonal entries of every diagonal block lie between 2 and 4.
All inputs are finite; a program needn't handle non-finite values.
Results may differ from the reference program's by a relative error of at most 0.035.
Values may be sent and summed in bfloat16 or wider, within the bound.
A program may use at most 64 MiB of HBM per device.

```python
import jax
import jax.numpy as jnp
from jax import lax

M = 512
R = 128
LEVELS = 3
LAYERS = 8


def diagonal_values(key):
    return jnp.exp(jax.random.uniform(jax.random.fold_in(key, 7), (LAYERS, M), jnp.float32, jnp.log(2.0), jnp.log(4.0)))


def coupling_draw(key, salt, toward):
    key_noise = jax.random.fold_in(jax.random.fold_in(key, salt), 0)
    key_ratio = jax.random.fold_in(jax.random.fold_in(key, salt), 2)
    values = diagonal_values(key)
    if toward < 0:
        neighbour = jnp.concatenate([values[:1], values[:-1]], axis=0)
    else:
        neighbour = jnp.concatenate([values[1:], values[-1:]], axis=0)
    coupling_ratio = jax.random.uniform(key_ratio, (LAYERS, M), jnp.float32, 0.41, 0.48)
    strength = -coupling_ratio * jnp.sqrt(values * neighbour)
    noise = jax.random.truncated_normal(key_noise, -4.0, 4.0, (LAYERS, M, M), jnp.float32)
    identity = jnp.eye(M, dtype=jnp.float32)
    block = noise * (0.45 / jnp.sqrt(M * 1.0)) * (1.0 - identity) + identity * strength[:, :, None]
    return block.astype(jnp.bfloat16)


def draw_lower_blocks(key, part):
    return coupling_draw(key, 21, -1)


def draw_upper_blocks(key, part):
    return coupling_draw(key, 31, 1)


def draw_diag_blocks(key, part):
    key_noise = jax.random.fold_in(jax.random.fold_in(key, 11), 0)
    diag_values = diagonal_values(key)
    noise = jax.random.truncated_normal(key_noise, -4.0, 4.0, (LAYERS, M, M), jnp.float32)
    identity = jnp.eye(M, dtype=jnp.float32)
    block = noise * (0.65 / jnp.sqrt(M * 1.0)) * (1.0 - identity) + identity * diag_values[:, :, None]
    return block.astype(jnp.bfloat16)


def levels(own_key, extent, cuts, low, high):
    factor_of, own = 1.0, jax.random.fold_in(own_key, 6)
    for position, blocks in cuts:
        draws = jnp.exp(jax.random.uniform(jax.random.fold_in(own, position), (blocks,), jnp.float32, low / len(cuts), high / len(cuts)))
        factor_of = factor_of * jnp.repeat(draws, extent[position] // blocks).reshape([-1 if axis == position else 1 for axis in range(len(extent))])
    return factor_of


def centred(own_key, extent, scale, most, cuts=(), kind=jnp.bfloat16):
    result = scale * jax.random.normal(own_key, extent, jnp.float32)
    if cuts:
        result = result * levels(own_key, extent, cuts, -0.22, 0.18)
    return jnp.clip(result, -most, most).astype(kind)


def setup_inputs(seed: int = 0) -> dict:
    arg_keys = jax.random.split(jax.random.key(seed), 5)
    return {
        "lower_blocks": draw_lower_blocks(jax.random.fold_in(arg_keys[4], 71), 0),
        "diag_blocks": draw_diag_blocks(jax.random.fold_in(arg_keys[4], 71), 0),
        "upper_blocks": draw_upper_blocks(jax.random.fold_in(arg_keys[4], 71), 0),
        "right_sides": centred(arg_keys[3], (LAYERS, M, R), 1.0, 6.0, ((0, 8), (1, 4))),
    }


def start_inverse(diag_block):
    inverse_diag = 1.0 / jnp.diagonal(diag_block).astype(jnp.float32)
    identity = jnp.eye(diag_block.shape[0], dtype=jnp.float32)
    guess = 2.0 * identity * inverse_diag[:, None] - inverse_diag[:, None] * diag_block.astype(jnp.float32) * inverse_diag[None, :]
    return guess.astype(jnp.bfloat16)


def invert(diag_block):
    first_guess = start_inverse(diag_block)
    product = jnp.dot(first_guess, diag_block, preferred_element_type=jnp.float32).astype(jnp.bfloat16)
    second = 2.0 * first_guess.astype(jnp.float32) - jnp.dot(product, first_guess, preferred_element_type=jnp.float32)
    return second.astype(jnp.bfloat16)


def solve_products(operands):
    diag_block, stacked = operands
    return jnp.dot(invert(diag_block), stacked, preferred_element_type=jnp.float32).astype(jnp.bfloat16)


def couple(operands):
    left_side, right_side = operands
    return jnp.dot(left_side, right_side, preferred_element_type=jnp.float32)


def eliminate(lower_rows, diag_rows, upper_rows, rhs_rows, terms_left, terms_right, order_size):
    new_lower = (-terms_left[..., :order_size]).astype(jnp.bfloat16)
    new_diag = (diag_rows.astype(jnp.float32) - terms_left[..., order_size:2 * order_size] - terms_right[..., :order_size]).astype(jnp.bfloat16)
    new_upper = (-terms_right[..., order_size:2 * order_size]).astype(jnp.bfloat16)
    new_rhs = (rhs_rows.astype(jnp.float32) - terms_left[..., 2 * order_size:] - terms_right[..., 2 * order_size:]).astype(jnp.bfloat16)
    return new_lower, new_diag, new_upper, new_rhs


def reference(lower_blocks, diag_blocks, upper_blocks, right_sides):
    order_size = lower_blocks.shape[1]
    for level_index in range(LEVELS):
        reach = 2 ** level_index
        stacked = jnp.concatenate([lower_blocks, upper_blocks, right_sides], axis=2)
        products = lax.map(solve_products, (diag_blocks, stacked))
        padding = jnp.zeros((reach,) + products.shape[1:], jnp.bfloat16)
        preceding = jnp.concatenate([padding, products[:-reach]], axis=0)
        following = jnp.concatenate([products[reach:], padding], axis=0)
        terms_left = lax.map(couple, (lower_blocks, preceding))
        terms_right = lax.map(couple, (upper_blocks, following))
        lower_blocks, diag_blocks, upper_blocks, right_sides = eliminate(lower_blocks, diag_blocks, upper_blocks, right_sides, terms_left, terms_right, order_size)
    return diag_blocks, right_sides
```

```python
import functools

import jax
import jax.numpy as jnp
from jax import lax
from jax.experimental import pallas as pl
from jax.experimental.pallas import tpu as pltpu
from jax.sharding import PartitionSpec as P

LEVELS = 3
LANES = 128
F32 = jnp.float32
BF16 = jnp.bfloat16


def dot_nn(a, b):
    return jnp.dot(a, b, preferred_element_type=F32)


def dot_nt(a, b):
    return lax.dot_general(a, b, (((1,), (1,)), ((), ())), preferred_element_type=F32)


def first_guess(diag_block):
    order = diag_block.shape[0]
    rows = lax.broadcasted_iota(jnp.int32, (order, order), 0)
    cols = lax.broadcasted_iota(jnp.int32, (order, order), 1)
    block = diag_block.astype(F32)
    eye = rows == cols
    only_diag = jnp.where(eye, block, 0.0)
    s_row = 1.0 / jnp.sum(only_diag, axis=0, keepdims=True)
    s_col = 1.0 / jnp.sum(only_diag, axis=1, keepdims=True)
    return (jnp.where(eye, 2.0 * s_row, 0.0) - s_col * block * s_row).astype(BF16)


def kernel(
    layers, panels, l_in, b_in, u_in, f_in, b_out, f_out,
    b_full, l_full, u_full, f_own, p_own, p_near, f_turn, b_turn, b_land, f_land,
    send_sems, recv_sems,
):
    blk, order = l_in.shape
    rhs = f_in.shape[1]
    fb = rhs // panels
    width = 2 * blk + fb
    layer = lax.axis_index("layer")
    panel = lax.axis_index("panel")
    parity = layer % 2
    counter = [0]
    sends = []

    def when(cond, action):
        if cond is None:
            action()
        else:
            pl.when(cond)(action)

    def exists(index):
        return jnp.logical_and(index >= 0, index < layers)

    def flip(index, offset):
        bit = 1
        while bit < panels:
            if offset & bit:
                index = index + bit - 2 * bit * ((index // bit) % 2)
            bit *= 2
        return index

    def copy(src, dst, where):
        n = counter[0]
        counter[0] += 1
        return pltpu.make_async_remote_copy(
            src_ref=src, dst_ref=dst, send_sem=send_sems.at[n], recv_sem=recv_sems.at[n],
            device_id=where, device_id_type=pl.DeviceIdType.MESH,
        )

    def launch(item, cond=None):
        when(cond, item.start)
        sends.append((item, cond))

    def own_rows(index):
        return pl.ds(pl.multiple_of(index * blk, blk), blk)

    mine = own_rows(panel)
    bits = []
    bit = panels // 2
    while bit >= 1:
        bits.append(bit)
        bit //= 2

    def gather_begin(source, full):
        plan, delivered, have = [], {}, [0]
        for bit in bits:
            for off in have:
                rows = own_rows(flip(panel, off))
                src = source if off == 0 else full.at[rows]
                item = copy(src, full.at[rows], {"panel": flip(panel, bit)})
                plan.append((off, item))
                delivered[bit ^ off] = item
            have = have + [o ^ bit for o in have]
        for off, item in plan:
            if off == 0:
                launch(item)
        return plan, delivered, set()

    def gather_forward(state):
        plan, delivered, done = state
        for off, item in plan:
            if off != 0:
                if off not in done:
                    delivered[off].wait_recv()
                    done.add(off)
                launch(item)

    def gather_end(state):
        plan, delivered, done = state
        for off in sorted(delivered):
            if off not in done:
                delivered[off].wait_recv()
                done.add(off)

    barrier = pltpu.get_barrier_semaphore()
    met = jnp.int32(0)
    for off in range(1, panels):
        pl.semaphore_signal(barrier, inc=1, device_id={"panel": (panel + off) % panels})
        met = met + 1
    partner = layer + 1 - 2 * parity
    others = [partner]
    for k in range(1, LEVELS):
        others += [layer - 2**k, layer + 2**k]
    for other in others:
        there = exists(other)

        def greet(other=other):
            pl.semaphore_signal(barrier, inc=1, device_id={"layer": other})

        pl.when(there)(greet)
        met = met + there.astype(jnp.int32)
    pl.semaphore_wait(barrier, met)

    state_b = gather_begin(b_in, b_full.at[0])
    f_turn[...] = f_in[...].T
    state_l = gather_begin(l_in, l_full.at[0])
    state_u = gather_begin(u_in, u_full.at[0])

    def f_rows(index):
        return pl.ds(pl.multiple_of(index * fb, fb), fb)

    f_items = []
    for off in range(1, panels):
        to = (panel + off) % panels
        item = copy(f_turn.at[f_rows(to)], f_own.at[0, :, mine], {"panel": to})
        launch(item)
        f_items.append(item)
    f_own[0, :, mine] = f_turn[f_rows(panel), :]
    b_full[0, mine, :] = b_in[...]
    l_full[0, mine, :] = l_in[...]
    u_full[0, mine, :] = u_in[...]

    for k in range(LEVELS):
        for slot, near in ((0, layer - 2**k), (1, layer + 2**k)):

            def clear(k=k, slot=slot):
                p_near[k, slot] = jnp.zeros((width, order), BF16)

            pl.when(jnp.logical_not(exists(near)))(clear)

    part_a = slice(0, blk)
    part_u = slice(blk + fb, width)
    part_af = slice(0, blk + fb)
    part_fu = slice(blk, width)

    for k in range(LEVELS):
        reach = 2**k
        last = k == LEVELS - 1
        gather_forward(state_b)
        gather_end(state_b)
        bt = b_full[k]
        guess = first_guess(bt)
        if k == 0:
            half = dot_nn(guess, bt).astype(BF16)
            gather_forward(state_l)
            inverse = (2.0 * guess.astype(F32) - dot_nn(half, guess)).astype(BF16)
            gather_forward(state_u)
            gather_end(state_l)
            gather_end(state_u)
            for item in f_items:
                item.wait_recv()
            own_l = l_full[0, :, mine].T
            own_u = u_full[0, :, mine].T
            own_b = b_full[0, :, mine].T
        else:
            half = dot_nn(bt, guess).astype(BF16)
            inverse = (2.0 * guess.astype(F32) - dot_nn(guess, half)).astype(BF16)
            own_l = l_full[k, mine, :]
            own_u = u_full[k, mine, :]
            own_b = b_full[k, mine, :]
        own_f = f_own[k]
        dot = dot_nt if k == 0 else dot_nn
        stacked = jnp.concatenate([own_l, own_f, own_u], axis=0)
        p_own[k] = dot(stacked, inverse).astype(BF16)

        arrivals = {0: [], 1: []}
        if k == 0:
            relays = []
            for part in (part_af, part_u):
                rows = pl.ds(part.start, part.stop - part.start)
                item = copy(
                    p_own.at[0, rows], p_near.at[0, parity, rows], {"layer": partner}
                )
                launch(item)
                relays.append((rows, item))
            onward = layer + 2 - 4 * parity
            origin = layer - 2 + 4 * parity
            late = []
            for rows, item in relays:
                item.wait_recv()
                again = copy(
                    p_near.at[0, 1 - parity, rows], p_near.at[0, parity, rows],
                    {"layer": onward},
                )
                launch(again, exists(onward))
                late.append(again)
            for again in late:
                pl.when(exists(origin))(again.wait_recv)
        else:
            parts = {0: (part_af, part_u), 1: (part_af, part_u)}
            if last:
                parts = {0: (part_fu,), 1: (part_af,)}
            for index in range(max(len(parts[0]), len(parts[1]))):
                for slot, to, origin in (
                    (0, layer + reach, layer - reach),
                    (1, layer - reach, layer + reach),
                ):
                    part = parts[slot][index]
                    rows = pl.ds(part.start, part.stop - part.start)
                    item = copy(p_own.at[k, rows], p_near.at[k, slot, rows], {"layer": to})
                    launch(item, exists(to))
                    arrivals[slot].append((item, exists(origin)))
            gather_forward(state_l)
            gather_forward(state_u)
            gather_end(state_l)
            gather_end(state_u)
            for slot in (0, 1):
                for item, cond in arrivals[slot]:
                    pl.when(cond)(item.wait_recv)

        left = dot(p_near[k, 0, part_fu, :], l_full[k])
        right = dot(p_near[k, 1, part_af, :], u_full[k])
        new_b = (own_b.astype(F32) - left[fb:] - right[:blk]).astype(BF16)
        new_f = (own_f.astype(F32) - left[:fb] - right[blk:]).astype(BF16)
        if not last:
            b_full[k + 1, mine, :] = new_b
            f_own[k + 1] = new_f
            new_l = -dot(p_near[k, 0, part_a, :], l_full[k])
            l_full[k + 1, mine, :] = new_l.astype(BF16)
            state_b = gather_begin(b_full.at[k + 1, mine], b_full.at[k + 1])
            new_u = -dot(p_near[k, 1, part_u, :], u_full[k])
            u_full[k + 1, mine, :] = new_u.astype(BF16)
            state_l = gather_begin(l_full.at[k + 1, mine], l_full.at[k + 1])
            state_u = gather_begin(u_full.at[k + 1, mine], u_full.at[k + 1])
        else:
            f_own[k + 1] = new_f
            b_turn[...] = new_b.T

    landings = []
    for off in range(1, panels):
        to = (panel + off) % panels
        item = copy(b_turn.at[own_rows(to)], b_land.at[:, mine], {"panel": to})
        launch(item)
        landings.append(item)
        item = copy(
            f_own.at[LEVELS, :, own_rows(to)], f_land.at[f_rows(panel)], {"panel": to}
        )
        launch(item)
        landings.append(item)
    b_land[:, mine] = b_turn[mine, :]
    f_land[f_rows(panel), :] = f_own[LEVELS, :, mine]
    for item in landings:
        item.wait_recv()
    b_out[...] = b_land[...]
    f_out[...] = f_land[...].T
    for item, cond in sends:
        when(cond, item.wait_send)


def on_device_kernel(layers, panels, lower_blocks, diag_blocks, upper_blocks, right_sides):
    _, blk, order = lower_blocks.shape
    rhs = right_sides.shape[2]
    fb = rhs // panels
    width = 2 * blk + fb
    copies = 160
    vmem = pl.BlockSpec(memory_space=pltpu.VMEM)
    new_diag, new_rhs = pl.pallas_call(
        functools.partial(kernel, layers, panels),
        out_shape=(
            jax.ShapeDtypeStruct((blk, order), BF16),
            jax.ShapeDtypeStruct((blk, rhs), BF16),
        ),
        in_specs=[vmem] * 4,
        out_specs=(vmem, vmem),
        scratch_shapes=[
            pltpu.VMEM((LEVELS, order, order), BF16),
            pltpu.VMEM((LEVELS, order, order), BF16),
            pltpu.VMEM((LEVELS, order, order), BF16),
            pltpu.VMEM((LEVELS + 1, fb, order), BF16),
            pltpu.VMEM((LEVELS, width, order), BF16),
            pltpu.VMEM((LEVELS, 2, width, order), BF16),
            pltpu.VMEM((rhs, blk), BF16),
            pltpu.VMEM((order, blk), BF16),
            pltpu.VMEM((blk, order), BF16),
            pltpu.VMEM((rhs, blk), BF16),
            pltpu.SemaphoreType.DMA((copies,)),
            pltpu.SemaphoreType.DMA((copies,)),
        ],
        compiler_params=pltpu.CompilerParams(collective_id=0, has_side_effects=True),
    )(lower_blocks[0], diag_blocks[0], upper_blocks[0], right_sides[0])
    return new_diag[None], new_rhs[None]


def from_behind(shard, axis, by):
    size = lax.axis_size(axis)
    pairs = [(i, i + by) for i in range(size) if 0 <= i + by < size]
    return lax.ppermute(shard, axis, pairs)


def start_inverse(diag_block):
    inverse_diag = 1.0 / jnp.diagonal(diag_block).astype(F32)
    identity = jnp.eye(diag_block.shape[0], dtype=F32)
    guess = (
        2.0 * identity * inverse_diag[:, None]
        - inverse_diag[:, None] * diag_block.astype(F32) * inverse_diag[None, :]
    )
    return guess.astype(BF16)


def eliminate(diag_rows, rhs_rows, terms_left, terms_right, order):
    new_lower = (-terms_left[..., :order]).astype(BF16)
    new_diag = (
        diag_rows.astype(F32) - terms_left[..., order : 2 * order] - terms_right[..., :order]
    ).astype(BF16)
    new_upper = (-terms_right[..., order : 2 * order]).astype(BF16)
    new_rhs = (
        rhs_rows.astype(F32) - terms_left[..., 2 * order :] - terms_right[..., 2 * order :]
    ).astype(BF16)
    return new_lower, new_diag, new_upper, new_rhs


def on_device_narrow(lower_blocks, diag_blocks, upper_blocks, right_sides):
    lower_rows, diag_rows = lower_blocks[0], diag_blocks[0]
    upper_rows, rhs_rows = upper_blocks[0], right_sides[0]
    order = lower_rows.shape[1]
    for level_index in range(LEVELS):
        reach = 2**level_index
        full_diag, full_lower, full_upper, full_rhs = (
            lax.all_gather(rows, "panel", axis=0, tiled=True)
            for rows in (diag_rows, lower_rows, upper_rows, rhs_rows)
        )
        stacked = jnp.concatenate([full_lower, full_upper, full_rhs], axis=1)
        guess = start_inverse(full_diag)
        product = dot_nn(guess, full_diag).astype(BF16)
        inverse = (2.0 * guess.astype(F32) - dot_nn(product, guess)).astype(BF16)
        solved = dot_nn(inverse, stacked).astype(BF16)
        coupling_next = from_behind(lower_rows, "layer", -reach)
        coupling_prev = from_behind(upper_rows, "layer", reach)
        partial_next = dot_nn(coupling_next, solved).astype(BF16)
        partial_prev = dot_nn(coupling_prev, solved).astype(BF16)
        terms_left = from_behind(partial_next, "layer", reach).astype(F32)
        terms_right = from_behind(partial_prev, "layer", -reach).astype(F32)
        lower_rows, diag_rows, upper_rows, rhs_rows = eliminate(
            diag_rows, rhs_rows, terms_left, terms_right, order
        )
    return diag_rows[None], rhs_rows[None]


def solution(mesh):
    layers, panels = mesh.shape["layer"], mesh.shape["panel"]
    spec = P("layer", "panel", None)

    def on_device(lower_blocks, diag_blocks, upper_blocks, right_sides):
        blk = lower_blocks.shape[1]
        fb = right_sides.shape[2] // panels
        aligned = blk % LANES == 0 and fb % 16 == 0 and panels & (panels - 1) == 0
        if aligned and layers % 2 == 0:
            return on_device_kernel(
                layers, panels, lower_blocks, diag_blocks, upper_blocks, right_sides
            )
        return on_device_narrow(lower_blocks, diag_blocks, upper_blocks, right_sides)

    return jax.shard_map(
        on_device, mesh=mesh, in_specs=(spec,) * 4, out_specs=(spec, spec), check_vma=False
    )
```

```python
import functools

import jax
import jax.numpy as jnp
from jax import lax
from jax.experimental import pallas as pl
from jax.experimental.pallas import tpu as pltpu
from jax.sharding import PartitionSpec as P

LEVELS = 3
LANES = 128
F32 = jnp.float32
BF16 = jnp.bfloat16


def dot_nn(a, b):
    return jnp.dot(a, b, preferred_element_type=F32)


def dot_nt(a, b):
    return lax.dot_general(a, b, (((1,), (1,)), ((), ())), preferred_element_type=F32)


def first_guess(diag_block):
    order = diag_block.shape[0]
    rows = lax.broadcasted_iota(jnp.int32, (order, order), 0)
    cols = lax.broadcasted_iota(jnp.int32, (order, order), 1)
    block = diag_block.astype(F32)
    eye = rows == cols
    only_diag = jnp.where(eye, block, 0.0)
    s_row = 1.0 / jnp.sum(only_diag, axis=0, keepdims=True)
    s_col = 1.0 / jnp.sum(only_diag, axis=1, keepdims=True)
    return (jnp.where(eye, 2.0 * s_row, 0.0) - s_col * block * s_row).astype(BF16)


def kernel(
    layers, panels, l_in, b_in, u_in, f_in, b_out, f_out,
    b_full, l_full, u_full, l_cols, u_cols, f_own, p_own, p_near, f_turn, b_turn, b_land, f_land,
    send_sems, recv_sems,
):
    blk, order = l_in.shape
    rhs = f_in.shape[1]
    fb = rhs // panels
    width = 2 * blk + fb
    layer = lax.axis_index("layer")
    panel = lax.axis_index("panel")
    parity = layer % 2
    counter = [0]
    sends = []

    def when(cond, action):
        if cond is None:
            action()
        else:
            pl.when(cond)(action)

    def exists(index):
        return jnp.logical_and(index >= 0, index < layers)

    def flip(index, offset):
        bit = 1
        while bit < panels:
            if offset & bit:
                index = index + bit - 2 * bit * ((index // bit) % 2)
            bit *= 2
        return index

    def copy(src, dst, where):
        n = counter[0]
        counter[0] += 1
        return pltpu.make_async_remote_copy(
            src_ref=src, dst_ref=dst, send_sem=send_sems.at[n], recv_sem=recv_sems.at[n],
            device_id=where, device_id_type=pl.DeviceIdType.MESH,
        )

    def launch(item, cond=None):
        when(cond, item.start)
        sends.append((item, cond))

    def own_rows(index):
        return pl.ds(pl.multiple_of(index * blk, blk), blk)

    mine = own_rows(panel)
    bits = []
    bit = panels // 2
    while bit >= 1:
        bits.append(bit)
        bit //= 2

    def gather_begin(source, full, cond=None):
        plan, delivered, have = [], {}, [0]
        for bit in bits:
            for off in have:
                rows = own_rows(flip(panel, off))
                src = source if off == 0 else full.at[rows]
                item = copy(src, full.at[rows], {"panel": flip(panel, bit)})
                plan.append((off, item))
                delivered[bit ^ off] = item
            have = have + [o ^ bit for o in have]
        for off, item in plan:
            if off == 0:
                launch(item, cond)
        return plan, delivered, set(), cond

    def gather_forward(state):
        plan, delivered, done, cond = state
        for off, item in plan:
            if off != 0:
                if off not in done:
                    when(cond, delivered[off].wait_recv)
                    done.add(off)
                launch(item, cond)

    def gather_end(state):
        plan, delivered, done, cond = state
        for off in sorted(delivered):
            if off not in done:
                when(cond, delivered[off].wait_recv)
                done.add(off)

    barrier = pltpu.get_barrier_semaphore()
    met = jnp.int32(0)
    for off in range(1, panels):
        pl.semaphore_signal(barrier, inc=1, device_id={"panel": (panel + off) % panels})
        met = met + 1
    partner = layer + 1 - 2 * parity
    others = [partner]
    for k in range(1, LEVELS):
        others += [layer - 2**k, layer + 2**k]
    for other in others:
        there = exists(other)

        def greet(other=other):
            pl.semaphore_signal(barrier, inc=1, device_id={"layer": other})

        pl.when(there)(greet)
        met = met + there.astype(jnp.int32)
    pl.semaphore_wait(barrier, met)

    state_b = gather_begin(b_in, b_full.at[0])
    f_turn[...] = f_in[...].T
    col_items = []
    for source, target in ((l_in, l_cols), (u_in, u_cols)):
        for off in range(1, panels):
            to = flip(panel, panels - off)
            item = copy(source.at[:, own_rows(to)], target.at[mine], {"panel": to})
            launch(item)
            col_items.append(item)

    def f_rows(index):
        return pl.ds(pl.multiple_of(index * fb, fb), fb)

    for off in range(1, panels):
        to = flip(panel, panels - off)
        item = copy(f_turn.at[f_rows(to)], f_own.at[0, :, mine], {"panel": to})
        launch(item)
        col_items.append(item)
    state_l = gather_begin(l_in, l_full.at[0])
    state_u = gather_begin(u_in, u_full.at[0])
    f_own[0, :, mine] = f_turn[f_rows(panel), :]
    b_full[0, mine, :] = b_in[...]
    l_full[0, mine, :] = l_in[...]
    u_full[0, mine, :] = u_in[...]
    l_cols[mine, :] = l_in[:, mine]
    u_cols[mine, :] = u_in[:, mine]

    for k in range(LEVELS):
        for slot, near, full in ((0, layer - 2**k, l_full), (1, layer + 2**k, u_full)):

            def clear(k=k, slot=slot, full=full):
                p_near[k, slot] = jnp.zeros((width, order), BF16)
                if k == LEVELS - 1:
                    full[k] = jnp.zeros((order, order), BF16)

            pl.when(jnp.logical_not(exists(near)))(clear)

    part_a = slice(0, blk)
    part_u = slice(blk + fb, width)
    part_af = slice(0, blk + fb)
    part_fu = slice(blk, width)

    def wait_all(items):
        for item, cond in items:
            when(cond, item.wait_recv)

    for k in range(LEVELS):
        reach = 2**k
        last = k == LEVELS - 1
        gather_forward(state_b)
        gather_end(state_b)
        bt = b_full[k]
        guess = first_guess(bt)
        if k == 0:
            half = dot_nn(guess, bt).astype(BF16)
            inverse = (2.0 * guess.astype(F32) - dot_nn(half, guess)).astype(BF16)
            for item in col_items:
                item.wait_recv()
            own_l = l_cols[...].T
            own_u = u_cols[...].T
            own_b = b_full[0, :, mine].T
        else:
            half = dot_nn(bt, guess).astype(BF16)
            inverse = (2.0 * guess.astype(F32) - dot_nn(guess, half)).astype(BF16)
            own_l = l_full[k, mine, :]
            own_u = u_full[k, mine, :]
            own_b = b_full[k, mine, :]
        own_f = f_own[k]
        dot = dot_nt if k == 0 else dot_nn
        stacked = jnp.concatenate([own_l, own_f, own_u], axis=0)
        p_own[k] = dot(stacked, inverse).astype(BF16)

        first, second = [], []
        if k == 0:
            onward = layer + 2 - 4 * parity
            origin = layer - 2 + 4 * parity
            piece = blk // 2
            plan = []
            for base in (parity * (blk + fb), (1 - parity) * (blk + fb)):
                for start in (0, piece):
                    plan.append(pl.ds(pl.multiple_of(base + start, 16), piece))
            plan.append(pl.ds(blk, fb))
            direct = []
            for rows in plan:
                item = copy(p_own.at[0, rows], p_near.at[0, parity, rows], {"layer": partner})
                launch(item)
                direct.append(item)
            relays = []
            for index, rows in enumerate(plan):
                if index < 4:
                    base = (1 - parity if index < 2 else parity) * (blk + fb)
                    rows = pl.ds(pl.multiple_of(base + (index % 2) * piece, 16), piece)
                again = copy(
                    p_near.at[0, 1 - parity, rows], p_near.at[0, parity, rows],
                    {"layer": onward},
                )
                relays.append(again)
            for index in (0, 1):
                direct[index].wait_recv()
                launch(relays[index], exists(onward))
            gather_forward(state_l)
            for index in (2, 3):
                direct[index].wait_recv()
                launch(relays[index], exists(onward))
            gather_forward(state_u)
            direct[4].wait_recv()
            launch(relays[4], exists(onward))
            first = [(relays[index], exists(origin)) for index in (0, 1)]
            second = [(relays[index], exists(origin)) for index in (2, 3, 4)]
        else:
            stages = (((0, part_u), (1, part_a)), ((0, part_af), (1, part_fu)))
            if last:
                stages = (((0, part_fu), (1, part_af)),)
            for stage, group in zip(stages, (first, second)):
                for slot, part in stage:
                    to = layer + reach if slot == 0 else layer - reach
                    origin = layer - reach if slot == 0 else layer + reach
                    rows = pl.ds(part.start, part.stop - part.start)
                    item = copy(p_own.at[k, rows], p_near.at[k, slot, rows], {"layer": to})
                    launch(item, exists(to))
                    group.append((item, exists(origin)))
            gather_forward(state_l)
            gather_forward(state_u)
        gather_end(state_l)
        gather_end(state_u)
        wait_all(first)
        if last:
            left = dot(p_near[k, 0, part_fu, :], l_full[k])
            right = dot(p_near[k, 1, part_af, :], u_full[k])
            new_b = (own_b.astype(F32) - left[fb:] - right[:blk]).astype(BF16)
            b_turn[...] = new_b.T
            new_f = (own_f.astype(F32) - left[:fb] - right[blk:]).astype(BF16)
            f_own[k + 1] = new_f
        else:
            left = dot(p_near[k, 0, part_u, :], l_full[k])
            right = dot(p_near[k, 1, part_a, :], u_full[k])
            new_b = (own_b.astype(F32) - left - right).astype(BF16)
            b_full[k + 1, mine, :] = new_b
            state_b = gather_begin(b_full.at[k + 1, mine], b_full.at[k + 1])
            wait_all(second)
            before_last = k + 1 == LEVELS - 1
            ahead = 2 ** (k + 1)
            left = dot(p_near[k, 0, part_af, :], l_full[k])
            l_full[k + 1, mine, :] = (-left[:blk]).astype(BF16)
            state_l = gather_begin(
                l_full.at[k + 1, mine], l_full.at[k + 1],
                exists(layer - ahead) if before_last else None,
            )
            right = dot(p_near[k, 1, part_fu, :], u_full[k])
            u_full[k + 1, mine, :] = (-right[fb:]).astype(BF16)
            state_u = gather_begin(
                u_full.at[k + 1, mine], u_full.at[k + 1],
                exists(layer + ahead) if before_last else None,
            )
            f_own[k + 1] = (own_f.astype(F32) - left[blk:] - right[:fb]).astype(BF16)

    landings = []
    for off in range(1, panels):
        to = (panel + off) % panels
        item = copy(b_turn.at[own_rows(to)], b_land.at[:, mine], {"panel": to})
        launch(item)
        landings.append(item)
        item = copy(
            f_own.at[LEVELS, :, own_rows(to)], f_land.at[f_rows(panel)], {"panel": to}
        )
        launch(item)
        landings.append(item)
    b_land[:, mine] = b_turn[mine, :]
    f_land[f_rows(panel), :] = f_own[LEVELS, :, mine]
    for item in landings:
        item.wait_recv()
    b_out[...] = b_land[...]
    f_out[...] = f_land[...].T
    for item, cond in sends:
        when(cond, item.wait_send)


def on_device_kernel(layers, panels, lower_blocks, diag_blocks, upper_blocks, right_sides):
    _, blk, order = lower_blocks.shape
    rhs = right_sides.shape[2]
    fb = rhs // panels
    width = 2 * blk + fb
    copies = 160
    vmem = pl.BlockSpec(memory_space=pltpu.VMEM)
    new_diag, new_rhs = pl.pallas_call(
        functools.partial(kernel, layers, panels),
        out_shape=(
            jax.ShapeDtypeStruct((blk, order), BF16),
            jax.ShapeDtypeStruct((blk, rhs), BF16),
        ),
        in_specs=[vmem] * 4,
        out_specs=(vmem, vmem),
        scratch_shapes=[
            pltpu.VMEM((LEVELS, order, order), BF16),
            pltpu.VMEM((LEVELS, order, order), BF16),
            pltpu.VMEM((LEVELS, order, order), BF16),
            pltpu.VMEM((order, blk), BF16),
            pltpu.VMEM((order, blk), BF16),
            pltpu.VMEM((LEVELS + 1, fb, order), BF16),
            pltpu.VMEM((LEVELS, width, order), BF16),
            pltpu.VMEM((LEVELS, 2, width, order), BF16),
            pltpu.VMEM((rhs, blk), BF16),
            pltpu.VMEM((order, blk), BF16),
            pltpu.VMEM((blk, order), BF16),
            pltpu.VMEM((rhs, blk), BF16),
            pltpu.SemaphoreType.DMA((copies,)),
            pltpu.SemaphoreType.DMA((copies,)),
        ],
        compiler_params=pltpu.CompilerParams(collective_id=0, has_side_effects=True),
    )(lower_blocks[0], diag_blocks[0], upper_blocks[0], right_sides[0])
    return new_diag[None], new_rhs[None]


def from_behind(shard, axis, by):
    size = lax.axis_size(axis)
    pairs = [(i, i + by) for i in range(size) if 0 <= i + by < size]
    return lax.ppermute(shard, axis, pairs)


def start_inverse(diag_block):
    inverse_diag = 1.0 / jnp.diagonal(diag_block).astype(F32)
    identity = jnp.eye(diag_block.shape[0], dtype=F32)
    guess = (
        2.0 * identity * inverse_diag[:, None]
        - inverse_diag[:, None] * diag_block.astype(F32) * inverse_diag[None, :]
    )
    return guess.astype(BF16)


def eliminate(diag_rows, rhs_rows, terms_left, terms_right, order):
    new_lower = (-terms_left[..., :order]).astype(BF16)
    new_diag = (
        diag_rows.astype(F32) - terms_left[..., order : 2 * order] - terms_right[..., :order]
    ).astype(BF16)
    new_upper = (-terms_right[..., order : 2 * order]).astype(BF16)
    new_rhs = (
        rhs_rows.astype(F32) - terms_left[..., 2 * order :] - terms_right[..., 2 * order :]
    ).astype(BF16)
    return new_lower, new_diag, new_upper, new_rhs


def on_device_narrow(lower_blocks, diag_blocks, upper_blocks, right_sides):
    lower_rows, diag_rows = lower_blocks[0], diag_blocks[0]
    upper_rows, rhs_rows = upper_blocks[0], right_sides[0]
    order = lower_rows.shape[1]
    for level_index in range(LEVELS):
        reach = 2**level_index
        full_diag, full_lower, full_upper, full_rhs = (
            lax.all_gather(rows, "panel", axis=0, tiled=True)
            for rows in (diag_rows, lower_rows, upper_rows, rhs_rows)
        )
        stacked = jnp.concatenate([full_lower, full_upper, full_rhs], axis=1)
        guess = start_inverse(full_diag)
        product = dot_nn(guess, full_diag).astype(BF16)
        inverse = (2.0 * guess.astype(F32) - dot_nn(product, guess)).astype(BF16)
        solved = dot_nn(inverse, stacked).astype(BF16)
        coupling_next = from_behind(lower_rows, "layer", -reach)
        coupling_prev = from_behind(upper_rows, "layer", reach)
        partial_next = dot_nn(coupling_next, solved).astype(BF16)
        partial_prev = dot_nn(coupling_prev, solved).astype(BF16)
        terms_left = from_behind(partial_next, "layer", reach).astype(F32)
        terms_right = from_behind(partial_prev, "layer", -reach).astype(F32)
        lower_rows, diag_rows, upper_rows, rhs_rows = eliminate(
            diag_rows, rhs_rows, terms_left, terms_right, order
        )
    return diag_rows[None], rhs_rows[None]


def solution(mesh):
    layers, panels = mesh.shape["layer"], mesh.shape["panel"]
    spec = P("layer", "panel", None)

    def on_device(lower_blocks, diag_blocks, upper_blocks, right_sides):
        blk = lower_blocks.shape[1]
        fb = right_sides.shape[2] // panels
        aligned = blk % LANES == 0 and fb % 16 == 0 and panels & (panels - 1) == 0
        if aligned and layers % 2 == 0:
            return on_device_kernel(
                layers, panels, lower_blocks, diag_blocks, upper_blocks, right_sides
            )
        return on_device_narrow(lower_blocks, diag_blocks, upper_blocks, right_sides)

    return jax.shard_map(
        on_device, mesh=mesh, in_specs=(spec,) * 4, out_specs=(spec, spec), check_vma=False
    )
```

```python
import functools

import jax
import jax.numpy as jnp
from jax import lax
from jax.experimental import pallas as pl
from jax.experimental.pallas import tpu as pltpu
from jax.sharding import PartitionSpec as P

LEVELS = 3
LANES = 128
PIECES = 2
F32 = jnp.float32
BF16 = jnp.bfloat16


def dot_nn(a, b):
    return jnp.dot(a, b, preferred_element_type=F32)


def dot_nt(a, b):
    return lax.dot_general(a, b, (((1,), (1,)), ((), ())), preferred_element_type=F32)


def first_guess(diag_block):
    order = diag_block.shape[0]
    rows = lax.broadcasted_iota(jnp.int32, (order, order), 0)
    cols = lax.broadcasted_iota(jnp.int32, (order, order), 1)
    block = diag_block.astype(F32)
    eye = rows == cols
    only_diag = jnp.where(eye, block, 0.0)
    s_row = 1.0 / jnp.sum(only_diag, axis=0, keepdims=True)
    s_col = 1.0 / jnp.sum(only_diag, axis=1, keepdims=True)
    return (jnp.where(eye, 2.0 * s_row, 0.0) - s_col * block * s_row).astype(BF16)


def kernel(
    layers, panels, l_hbm, b_hbm, u_hbm, f_hbm, b_out, f_out, l_in, b_in, u_in, f_in,
    b_full, l_full, u_full, l_cols, u_cols, f_own, p_own, p_near, f_turn, b_last, b_land, f_land,
    send_sems, recv_sems, load_sems,
):
    blk, order = l_in.shape
    rhs = f_in.shape[1]
    fb = rhs // panels
    width = 2 * blk + fb
    layer = lax.axis_index("layer")
    panel = lax.axis_index("panel")
    parity = layer % 2
    counter = [0]
    sends = []

    def when(cond, action):
        if cond is None:
            action()
        else:
            pl.when(cond)(action)

    def exists(index):
        return jnp.logical_and(index >= 0, index < layers)

    def flip(index, offset):
        bit = 1
        while bit < panels:
            if offset & bit:
                index = index + bit - 2 * bit * ((index // bit) % 2)
            bit *= 2
        return index

    def copy(src, dst, where):
        n = counter[0]
        counter[0] += 1
        return pltpu.make_async_remote_copy(
            src_ref=src, dst_ref=dst, send_sem=send_sems.at[n], recv_sem=recv_sems.at[n],
            device_id=where, device_id_type=pl.DeviceIdType.MESH,
        )

    def launch(item, cond=None):
        when(cond, item.start)
        sends.append((item, cond))

    def own_rows(index):
        return pl.ds(pl.multiple_of(index * blk, blk), blk)

    mine = own_rows(panel)
    bits = []
    bit = panels // 2
    while bit >= 1:
        bits.append(bit)
        bit //= 2

    def gather_begin(source, full, cond=None, start=0, size=None):
        def piece(index):
            return pl.ds(pl.multiple_of(index * blk + start, 16), size or blk)

        plan, delivered, have = [], {}, [0]
        for bit in bits:
            for off in have:
                rows = piece(flip(panel, off))
                src = source if off == 0 else full.at[rows]
                item = copy(src, full.at[rows], {"panel": flip(panel, bit)})
                plan.append((off, item))
                delivered[bit ^ off] = item
            have = have + [o ^ bit for o in have]
        for off, item in plan:
            if off == 0:
                launch(item, cond)
        return plan, delivered, set(), cond

    def gather_forward(states):
        for state in states:
            forward_one(state)

    def gather_end(states):
        for state in states:
            end_one(state)

    def forward_one(state):
        plan, delivered, done, cond = state
        for off, item in plan:
            if off != 0:
                if off not in done:
                    when(cond, delivered[off].wait_recv)
                    done.add(off)
                launch(item, cond)

    def end_one(state):
        plan, delivered, done, cond = state
        for off in sorted(delivered):
            if off not in done:
                when(cond, delivered[off].wait_recv)
                done.add(off)

    loads = []
    for n, (src, dst) in enumerate(
        ((b_hbm, b_in), (l_hbm, l_in), (u_hbm, u_in), (f_hbm, f_in))
    ):
        loads.append(pltpu.make_async_copy(src, dst, load_sems.at[n]))
        loads[n].start()
    barrier = pltpu.get_barrier_semaphore()
    met = jnp.int32(0)
    for off in range(1, panels):
        pl.semaphore_signal(barrier, inc=1, device_id={"panel": (panel + off) % panels})
        met = met + 1
    partner = layer + 1 - 2 * parity
    others = [partner]
    for k in range(1, LEVELS):
        others += [layer - 2**k, layer + 2**k]
    for other in others:
        there = exists(other)

        def greet(other=other):
            pl.semaphore_signal(barrier, inc=1, device_id={"layer": other})

        pl.when(there)(greet)
        met = met + there.astype(jnp.int32)
    for item in loads:
        item.wait()
    pl.semaphore_wait(barrier, met)

    half_rows = blk // PIECES
    state_b = []
    for h in range(PIECES):
        state_b.append(
            gather_begin(
                b_in.at[pl.ds(h * half_rows, half_rows)], b_full.at[0], None,
                h * half_rows, half_rows,
            )
        )
    f_turn[...] = f_in[...].T
    col_items = []
    for source, target in ((l_in, l_cols), (u_in, u_cols)):
        for off in range(1, panels):
            to = flip(panel, panels - off)
            item = copy(source.at[:, own_rows(to)], target.at[mine], {"panel": to})
            launch(item)
            col_items.append(item)

    def f_rows(index):
        return pl.ds(pl.multiple_of(index * fb, fb), fb)

    for off in range(1, panels):
        to = flip(panel, panels - off)
        item = copy(f_turn.at[f_rows(to)], f_own.at[0, :, mine], {"panel": to})
        launch(item)
        col_items.append(item)
    state_l = [gather_begin(l_in, l_full.at[0])]
    state_u = [gather_begin(u_in, u_full.at[0])]
    f_own[0, :, mine] = f_turn[f_rows(panel), :]
    b_full[0, mine, :] = b_in[...]
    l_full[0, mine, :] = l_in[...]
    u_full[0, mine, :] = u_in[...]
    l_cols[mine, :] = l_in[:, mine]
    u_cols[mine, :] = u_in[:, mine]

    for k in range(LEVELS):
        for slot, near, full in ((0, layer - 2**k, l_full), (1, layer + 2**k, u_full)):

            def clear(k=k, slot=slot, full=full):
                p_near[k, slot] = jnp.zeros((width, order), BF16)
                if k == LEVELS - 1:
                    full[k] = jnp.zeros((order, order), BF16)

            pl.when(jnp.logical_not(exists(near)))(clear)

    half_a = [slice(h * half_rows, (h + 1) * half_rows) for h in range(PIECES)]
    half_u = [slice(blk + fb + p.start, blk + fb + p.stop) for p in half_a]
    part_f = slice(blk, blk + fb)

    def wait_all(items):
        for item, cond in items:
            when(cond, item.wait_recv)

    landings = []

    def land_f():
        for off in range(1, panels):
            to = flip(panel, panels - off)
            item = copy(
                f_own.at[LEVELS, :, own_rows(to)], f_land.at[f_rows(panel)], {"panel": to}
            )
            launch(item)
            landings.append(item)
        f_land[f_rows(panel), :] = f_own[LEVELS, :, mine]

    def land_b(h):
        target = pl.ds(pl.multiple_of(panel * blk + h * half_rows, 16), half_rows)
        for off in range(1, panels):
            to = flip(panel, panels - off)
            item = copy(
                b_last.at[pl.ds(h * half_rows, half_rows), own_rows(to)], b_land.at[target],
                {"panel": to},
            )
            launch(item)
            landings.append(item)
        b_land[target, :] = b_last[half_a[h], mine]

    for k in range(LEVELS):
        reach = 2**k
        last = k == LEVELS - 1
        if k == 0:
            gather_forward(state_b)
        gather_end(state_b)
        bt = b_full[k]
        guess = first_guess(bt)
        if k == 0:
            half = dot_nn(guess, bt).astype(BF16)
            inverse = (2.0 * guess.astype(F32) - dot_nn(half, guess)).astype(BF16)
            for item in col_items:
                item.wait_recv()
            own_l = l_cols[...].T
            own_u = u_cols[...].T
            own_b = b_full[0, :, mine].T
        else:
            own_l = l_full[k, mine, :]
            own_u = u_full[k, mine, :]
            own_b = b_full[k, mine, :]
        own_f = f_own[k]
        dot = dot_nt if k == 0 else dot_nn

        first, second, third = [[] for _ in half_a], [[] for _ in half_a], []
        if k == 0:
            stacked = jnp.concatenate([own_l, own_f, own_u], axis=0)
            p_own[0] = dot(stacked, inverse).astype(BF16)
            onward = layer + 2 - 4 * parity
            origin = layer - 2 + 4 * parity

            def pieces(side):
                plan = []
                for base in (side * (blk + fb), (1 - side) * (blk + fb)):
                    for part in half_a:
                        start = pl.multiple_of(base + part.start, 16)
                        plan.append(pl.ds(start, half_rows))
                plan.append(pl.ds(blk, fb))
                return plan

            direct, relays = [], []
            for rows in pieces(parity):
                item = copy(p_own.at[0, rows], p_near.at[0, parity, rows], {"layer": partner})
                launch(item)
                direct.append(item)
            for rows in pieces(1 - parity):
                relays.append(
                    copy(
                        p_near.at[0, 1 - parity, rows], p_near.at[0, parity, rows],
                        {"layer": onward},
                    )
                )
            for index, (item, again) in enumerate(zip(direct, relays)):
                if index == PIECES:
                    gather_forward(state_l)
                item.wait_recv()
                launch(again, exists(onward))
            gather_forward(state_u)
            for h in range(PIECES):
                first[h].append((relays[h], exists(origin)))
                second[h].append((relays[PIECES + h], exists(origin)))
            third.append((relays[2 * PIECES], exists(origin)))
        else:

            def exchange(slot, part, group):
                to = layer + reach if slot == 0 else layer - reach
                origin = layer - reach if slot == 0 else layer + reach
                rows = pl.ds(part.start, part.stop - part.start)
                item = copy(p_own.at[k, rows], p_near.at[k, slot, rows], {"layer": to})
                launch(item, exists(to))
                group.append((item, exists(origin)))

            scaled = dot_nn(jnp.concatenate([own_l, own_f, own_u], axis=0), guess)
            back = dot_nn(scaled.astype(BF16), bt).astype(BF16)
            p_own[k] = (2.0 * scaled - dot_nn(back, guess)).astype(BF16)
            for h, (a, u) in enumerate(zip(half_a, half_u)):
                if h == 0:
                    if last:
                        exchange(0, part_f, third)
                        exchange(1, part_f, third)
                exchange(0, u, first[h])
                exchange(1, a, first[h])
            if not last:
                for h, (a, u) in enumerate(zip(half_a, half_u)):
                    exchange(0, a, second[h])
                    exchange(1, u, second[h])
                exchange(0, part_f, third)
                exchange(1, part_f, third)
            gather_forward(state_l)
            gather_forward(state_u)
        gather_end(state_l)
        gather_end(state_u)

        def new_rhs():
            wait_all(third)
            left = dot(p_near[k, 0, part_f, :], l_full[k])
            right = dot(p_near[k, 1, part_f, :], u_full[k])
            f_own[k + 1] = (own_f.astype(F32) - left - right).astype(BF16)

        def new_diag(h):
            wait_all(first[h])
            left = dot(p_near[k, 0, half_u[h], :], l_full[k])
            right = dot(p_near[k, 1, half_a[h], :], u_full[k])
            return (own_b[half_a[h]].astype(F32) - left - right).astype(BF16)

        def share(full, h, value, cond=None):
            rows = pl.ds(pl.multiple_of(panel * blk + h * half_rows, 16), half_rows)
            full[k + 1, rows, :] = value
            return gather_begin(
                full.at[k + 1, rows], full.at[k + 1], cond, h * half_rows, half_rows
            )

        if last:
            new_rhs()
            land_f()
            for h in range(PIECES):
                b_last[half_a[h], :] = new_diag(h)
                land_b(h)
        else:
            state_b, state_l, state_u = [], [], []
            for h in range(PIECES):
                state_b.append(share(b_full, h, new_diag(h)))
            before_last = k + 1 == LEVELS - 1
            ahead = 2 ** (k + 1)
            for h in range(PIECES):
                wait_all(second[h])
                value = -dot(p_near[k, 0, half_a[h], :], l_full[k])
                cond = exists(layer - ahead) if before_last else None
                state_l.append(share(l_full, h, value.astype(BF16), cond))
                value = -dot(p_near[k, 1, half_u[h], :], u_full[k])
                cond = exists(layer + ahead) if before_last else None
                state_u.append(share(u_full, h, value.astype(BF16), cond))
                if h > 0:
                    forward_one(state_b[h - 1])
            forward_one(state_b[PIECES - 1])
            new_rhs()

    for item in landings:
        item.wait_recv()
    b_out[...] = b_land[...]
    f_out[...] = f_land[...]
    for item, cond in sends:
        when(cond, item.wait_send)
    assert counter[0] == send_sems.shape[0]


def hand_over(turned_diag_in, turned_in, diag_out, rhs_out):
    diag_out[...] = turned_diag_in[...].T
    rhs_out[...] = turned_in[...].T


def on_device_kernel(layers, panels, lower_blocks, diag_blocks, upper_blocks, right_sides):
    _, blk, order = lower_blocks.shape
    rhs = right_sides.shape[2]
    fb = rhs // panels
    width = 2 * blk + fb
    peers, steps = panels - 1, LEVELS - 1
    copies = peers * (2 * PIECES + 6 + 3 * PIECES * steps)
    copies += 2 * (2 * PIECES + 1) * steps + 2 * (PIECES + 1)
    vmem = pl.BlockSpec(memory_space=pltpu.VMEM)
    new_diag, new_rhs = pl.pallas_call(
        functools.partial(kernel, layers, panels),
        out_shape=(
            jax.ShapeDtypeStruct((order, blk), BF16),
            jax.ShapeDtypeStruct((rhs, blk), BF16),
        ),
        in_specs=[pl.BlockSpec(memory_space=pl.ANY)] * 4,
        out_specs=(vmem, vmem),
        scratch_shapes=[
            pltpu.VMEM((blk, order), BF16),
            pltpu.VMEM((blk, order), BF16),
            pltpu.VMEM((blk, order), BF16),
            pltpu.VMEM((blk, rhs), BF16),
            pltpu.VMEM((LEVELS, order, order), BF16),
            pltpu.VMEM((LEVELS, order, order), BF16),
            pltpu.VMEM((LEVELS, order, order), BF16),
            pltpu.VMEM((order, blk), BF16),
            pltpu.VMEM((order, blk), BF16),
            pltpu.VMEM((LEVELS + 1, fb, order), BF16),
            pltpu.VMEM((LEVELS, width, order), BF16),
            pltpu.VMEM((LEVELS, 2, width, order), BF16),
            pltpu.VMEM((rhs, blk), BF16),
            pltpu.VMEM((blk, order), BF16),
            pltpu.VMEM((order, blk), BF16),
            pltpu.VMEM((rhs, blk), BF16),
            pltpu.SemaphoreType.DMA((copies,)),
            pltpu.SemaphoreType.DMA((copies,)),
            pltpu.SemaphoreType.DMA((4,)),
        ],
        compiler_params=pltpu.CompilerParams(collective_id=0, has_side_effects=True),
    )(lower_blocks[0], diag_blocks[0], upper_blocks[0], right_sides[0])
    new_diag, new_rhs = pl.pallas_call(
        hand_over,
        out_shape=(
            jax.ShapeDtypeStruct((blk, order), BF16),
            jax.ShapeDtypeStruct((blk, rhs), BF16),
        ),
        in_specs=[vmem] * 2,
        out_specs=(vmem, vmem),
    )(new_diag, new_rhs)
    return new_diag[None], new_rhs[None]


def from_behind(shard, axis, by):
    size = lax.axis_size(axis)
    pairs = [(i, i + by) for i in range(size) if 0 <= i + by < size]
    return lax.ppermute(shard, axis, pairs)


def start_inverse(diag_block):
    inverse_diag = 1.0 / jnp.diagonal(diag_block).astype(F32)
    identity = jnp.eye(diag_block.shape[0], dtype=F32)
    guess = (
        2.0 * identity * inverse_diag[:, None]
        - inverse_diag[:, None] * diag_block.astype(F32) * inverse_diag[None, :]
    )
    return guess.astype(BF16)


def eliminate(diag_rows, rhs_rows, terms_left, terms_right, order):
    new_lower = (-terms_left[..., :order]).astype(BF16)
    new_diag = (
        diag_rows.astype(F32) - terms_left[..., order : 2 * order] - terms_right[..., :order]
    ).astype(BF16)
    new_upper = (-terms_right[..., order : 2 * order]).astype(BF16)
    new_rhs = (
        rhs_rows.astype(F32) - terms_left[..., 2 * order :] - terms_right[..., 2 * order :]
    ).astype(BF16)
    return new_lower, new_diag, new_upper, new_rhs


def on_device_narrow(lower_blocks, diag_blocks, upper_blocks, right_sides):
    lower_rows, diag_rows = lower_blocks[0], diag_blocks[0]
    upper_rows, rhs_rows = upper_blocks[0], right_sides[0]
    order = lower_rows.shape[1]
    for level_index in range(LEVELS):
        reach = 2**level_index
        full_diag, full_lower, full_upper, full_rhs = (
            lax.all_gather(rows, "panel", axis=0, tiled=True)
            for rows in (diag_rows, lower_rows, upper_rows, rhs_rows)
        )
        stacked = jnp.concatenate([full_lower, full_upper, full_rhs], axis=1)
        guess = start_inverse(full_diag)
        product = dot_nn(guess, full_diag).astype(BF16)
        inverse = (2.0 * guess.astype(F32) - dot_nn(product, guess)).astype(BF16)
        solved = dot_nn(inverse, stacked).astype(BF16)
        coupling_next = from_behind(lower_rows, "layer", -reach)
        coupling_prev = from_behind(upper_rows, "layer", reach)
        partial_next = dot_nn(coupling_next, solved).astype(BF16)
        partial_prev = dot_nn(coupling_prev, solved).astype(BF16)
        terms_left = from_behind(partial_next, "layer", reach).astype(F32)
        terms_right = from_behind(partial_prev, "layer", -reach).astype(F32)
        lower_rows, diag_rows, upper_rows, rhs_rows = eliminate(
            diag_rows, rhs_rows, terms_left, terms_right, order
        )
    return diag_rows[None], rhs_rows[None]


def solution(mesh):
    layers, panels = mesh.shape["layer"], mesh.shape["panel"]
    spec = P("layer", "panel", None)

    def on_device(lower_blocks, diag_blocks, upper_blocks, right_sides):
        blk = lower_blocks.shape[1]
        fb = right_sides.shape[2] // panels
        aligned = blk % LANES == 0 and fb % 16 == 0 and blk // PIECES % 16 == 0 and panels & (panels - 1) == 0
        if aligned and layers % 2 == 0:
            return on_device_kernel(
                layers, panels, lower_blocks, diag_blocks, upper_blocks, right_sides
            )
        return on_device_narrow(lower_blocks, diag_blocks, upper_blocks, right_sides)

    return jax.shard_map(
        on_device, mesh=mesh, in_specs=(spec,) * 4, out_specs=(spec, spec), check_vma=False
    )
```
